256 devices in a mesh: layer: 4 (over y_lo, core), row: 8 (over x, y_hi), col: 8 (over z).
Axes of the slice: x: 4, y: 4 (y_hi: 2, y_lo: 2; y = y_hi * 2 + y_lo), z: 8, core: 2. Of those that a mesh axis runs over, the one named last changes fastest.
Arguments:
- integrals: bfloat16 [8192, 131072], P('row', ('layer', 'col')), may hold values from -0.015625 to 0.015625
- density: bfloat16 [131072, 1024], P(('layer', 'col'), 'row'), may hold values from -6 to 6
- mask_int: int32 [64, 1024], P('row', ('layer', 'col')), may hold values 0 or 1
- mask_den: int32 [1024, 8], P(('layer', 'col'), 'row'), may hold values 0 or 1
- owner_map: int32 [8, 64, 1], P('row'), may hold values from 0 to 31; in each aligned block of 64 rows (0 to 63, 64 to 127, ..., all dimensions but the last counted through in order) at most 4 rows name the same one
Outputs:
- owned: bfloat16 [8, 32, 4, 128, 128], P('row', ('layer', 'col'))
The draws below stay inside these ranges and needn't reach their ends.
Inputs may be any that keep to these rules, and one draw needn't show every extreme that they name: `owner_map`: among the 64 tiles of one row index no owner is named more than 4 times, a bound that some block reaches.
All inputs are finite; a program needn't handle non-finite values. No bound on the sum of `mask_int` or of `mask_den` on one device may be relied on, other than what follows from the above.
Results may differ from the reference program's by a relative error of at most 0.001.
Values may be sent and summed in bfloat16 or wider, within the bound.
No kernel may reach another device: no remote copies, remote signals or barrier semaphores. Data moves between devices by JAX's collectives and lax.ppermute only.
A program may use at most 128 MiB of HBM per device.

```python
import math
import jax
import jax.numpy as jnp
import numpy as np
from jax import lax

TILE = 128
TM = 8
CAP = 4
GROUP = 32
ROWTILES = 64
KTILES = 1024
COLTILES = 8
TILES = 64
N_ROW = 8


def with_ends(values, own_key, least, top_value):
    longest = values.shape.index(max(values.shape))
    spots = []
    for shift in (0, 1):
        where = [jax.random.randint(jax.random.fold_in(own_key, axis), (), 0, length) for axis, length in enumerate(values.shape)]
        where[longest] = (where[longest] + shift) % values.shape[longest]
        spots.append(tuple(where))
    return values.at[spots[0]].set(least).at[spots[1]].set(top_value)


def level_of(stream_key, dims, shards, smallest, largest):
    def one(dim, parts):
        heights = jax.random.uniform(jax.random.fold_in(jax.random.fold_in(stream_key, 6), dim), (parts,), jnp.float32, smallest / len(shards), largest / len(shards))
        return jnp.repeat(jnp.exp(heights), dims[dim] // parts).reshape((-1,) + (1,) * (len(dims) - dim - 1))

    factor_of = one(*shards[0])
    for cut in shards[1:]:
        factor_of = factor_of * one(*cut)
    return factor_of


def routed_block(own_key, own, number, rows, number_of, top, limit, skew):
    ranking = jax.random.permutation(own_key, number_of)
    crowded, usual = shares(number_of, rows * top, limit, skew, True), shares(number_of, rows * top, limit, skew, False)
    places = jnp.arange(number_of)

    def named(tallies, rotation):
        used = int((tallies > 0).sum())
        fixed = max(1, used // 4)
        moved = fixed + (places - fixed + rotation * (used - fixed)) % max(1, number_of - fixed)
        return jnp.zeros((number_of,), jnp.int32).at[ranking[jnp.where(places < fixed, places, moved)]].set(jnp.asarray(tallies, jnp.int32))

    tallies = jnp.where(number % 4 == 0, named(crowded, number // 4), named(usual, number - number // 4 - 1))
    mixed = jax.random.permutation(jax.random.fold_in(own, 3), number_of)
    giver, sink = mixed[0:number_of // 2 * 2:2], mixed[1:number_of // 2 * 2:2]
    room = jnp.minimum(tallies[giver] - 1, limit - tallies[sink]) // 2
    room = jnp.where((giver == ranking[0]) | (sink == ranking[0]) | (tallies[sink] == 0), 0, jnp.maximum(room, 0))
    moved = jax.random.randint(jax.random.fold_in(own, 4), (number_of // 2,), 0, 1 << 20) % (room + 1)
    tallies = tallies.at[giver].add(-moved).at[sink].add(moved)
    members = jnp.searchsorted(jnp.cumsum(tallies), jnp.arange(rows * top), side="right").astype(jnp.int32)
    table = members.reshape(top, rows).T
    table = table[jax.random.permutation(jax.random.fold_in(own, 1), rows)]
    rotation = jax.random.randint(jax.random.fold_in(own, 2), (rows, 1), 0, top)
    return jnp.take_along_axis(table, (jnp.arange(top)[None, :] + rotation) % top, axis=1)


def shares(amount, total, most, slope, full):
    loads = [(1 << 20) // math.isqrt(standing ** slope) + 1 for standing in range(1, amount + 1)]
    largest = most if full else min(most, max(-(-total // amount), total * loads[0] // sum(loads)))
    least = 1 if total - largest >= amount - 1 else 0
    holding, spare = [largest] + [least] * (amount - 1), total - largest - least * (amount - 1)
    while spare > 0:
        free = [i for i in range(1, amount) if holding[i] < largest] or [i for i in range(1, amount) if holding[i] < most]
        whole, budget = sum([loads[i] for i in free]), spare
        for i in free:
            more = min(most - holding[i], max(1, budget * loads[i] // whole), spare)
            holding[i] = holding[i] + more
            spare = spare - more
    return np.array(holding)


def normal_values(key, shape, scale, bound, pieces=(), held_as=jnp.bfloat16):
    result = scale * jax.random.normal(key, shape, jnp.float32)
    if pieces:
        result = result * level_of(key, shape, pieces, -0.22, 0.18)
    return jnp.clip(result, -bound, bound).astype(held_as)


def setup_inputs(seed: int = 0) -> dict:
    splits = jax.random.split(jax.random.key(seed), 6)
    integrals = normal_values(splits[0], (ROWTILES * TILE, KTILES * TILE), (KTILES * TILE) ** -0.5, 0.015625, ((0, 8), (1, 32)))
    density = normal_values(splits[1], (KTILES * TILE, COLTILES * TILE), 1.0, 6.0, ((0, 32), (1, 8)))
    mask_int = with_ends((jax.random.randint(splits[2], (ROWTILES, KTILES), 0, 5) < 3).astype(jnp.int32), jax.random.fold_in(splits[2], 1), 0, 1)
    mask_den = with_ends((jax.random.randint(splits[3], (KTILES, COLTILES), 0, 5) < 3).astype(jnp.int32), jax.random.fold_in(splits[3], 1), 0, 1)
    owner_map_keys = jax.random.split(jax.random.fold_in(splits[4], 1), N_ROW * TILES // TILES)
    owner_map_turns = jax.random.permutation(jax.random.fold_in(splits[4], 3), N_ROW * TILES // TILES)
    owner_map = jax.vmap(lambda own, number: routed_block(jax.random.fold_in(splits[4], 2), own, number, TILES, GROUP, 1, CAP, 2))(owner_map_keys, owner_map_turns).reshape((N_ROW, TILES, 1))
    return dict(integrals=integrals, density=density, mask_int=mask_int, mask_den=mask_den, owner_map=owner_map)


def apply_mask(block, mask):
    rows, cols = mask.shape
    shaped = block.reshape(rows, TILE, cols, TILE)
    return (shaped * mask.astype(jnp.bfloat16)[:, None, :, None]).reshape(block.shape)


def reference(integrals, density, mask_int, mask_den, owner_map):
    masked_density = apply_mask(density, mask_den)
    peers = jnp.arange(GROUP * CAP, dtype=jnp.int32)

    def one_row(items):
        block, mask, owners = items
        masked = apply_mask(block, mask)
        product = jnp.dot(masked, masked_density, preferred_element_type=jnp.float32)
        tiles = product.reshape(TM, TILE, COLTILES, TILE).transpose(0, 2, 1, 3).reshape(TILES, TILE * TILE)
        hits = (owners[:, None] == jnp.arange(GROUP, dtype=jnp.int32)[None, :]).astype(jnp.int32)
        slots = jnp.sum((jnp.cumsum(hits, axis=0) - hits) * hits, axis=1)
        place = ((owners[None, :] == (peers // CAP)[:, None]) & (slots[None, :] == (peers % CAP)[:, None])).astype(jnp.float32)
        placed = jnp.dot(place, tiles, precision=lax.Precision.HIGHEST, preferred_element_type=jnp.float32)
        return placed.astype(jnp.bfloat16).reshape(GROUP, CAP, TILE, TILE)

    return lax.map(one_row, (integrals.reshape(N_ROW, TM * TILE, KTILES * TILE), mask_int.reshape(N_ROW, TM, KTILES), owner_map.reshape(N_ROW, TILES)))
```

```python
import functools
import jax
import jax.numpy as jnp
from jax import lax
from jax.experimental import pallas as pl
from jax.experimental.pallas import tpu as pltpu
from jax.sharding import PartitionSpec as P

TILE = 128
CAP = 4
NX = 4
NZ = 8
ROWS = 8


def x_shift(step):
    return [(2 * x + h, 2 * ((x + step) % NX) + h) for x in range(NX) for h in range(2)]


Y_SWAP = [(2 * x + h, 2 * x + 1 - h) for x in range(NX) for h in range(2)]
CORE_SWAP = [(i, i ^ 1) for i in range(4)]
YLO_SWAP = [(i, i ^ 2) for i in range(4)]


def from_left(v):
    return lax.ppermute(v, "row", x_shift(1))


def from_right(v):
    return lax.ppermute(v, "row", x_shift(-1))


def from_pair(v):
    return lax.ppermute(v, "row", Y_SWAP)


def matmul_kernel(blocks, core_ref, a_ref, m_ref, *refs):
    n = sum(len(b) for b in blocks)
    pieces, (mine, other) = refs[:n], refs[n:]
    core = core_ref[0]
    i = 0
    for j, block in enumerate(blocks):
        acc = None
        for spans in block:
            at = 0
            for k0, k1 in spans:
                left = a_ref[:, k0:k1] * m_ref[0, :, k0:k1]
                part = jnp.dot(
                    left, pieces[i][at : at + k1 - k0, :], preferred_element_type=jnp.float32
                )
                acc = part if acc is None else acc + part
                at += k1 - k0
            i += 1
        half = acc.reshape(2, NZ, ROWS, TILE)

        @pl.when(core == 0)
        def _():
            mine[:, j, 0] = half[0]
            other[:, j, 0] = half[1]

        @pl.when(core == 1)
        def _():
            mine[:, j, 0] = half[1]
            other[:, j, 0] = half[0]


def matmul(core, a, row_mask, blocks):
    rows, depth = a.shape
    tiles = rows // TILE
    arrays = [v for b in blocks for v, _ in b]
    spans = [[s for _, s in b] for b in blocks]
    nb = len(blocks)
    out = jax.ShapeDtypeStruct((NZ, nb, tiles, ROWS, TILE), jnp.float32)
    out_spec = pl.BlockSpec((NZ, nb, 1, ROWS, TILE), lambda i, c: (0, 0, i, 0, 0))
    return pl.pallas_call(
        functools.partial(matmul_kernel, spans),
        out_shape=(out, out),
        grid_spec=pltpu.PrefetchScalarGridSpec(
            num_scalar_prefetch=1,
            grid=(tiles,),
            in_specs=[
                pl.BlockSpec((TILE, depth), lambda i, c: (i, 0)),
                pl.BlockSpec((1, 1, depth), lambda i, c: (i, 0, 0)),
            ]
            + [pl.BlockSpec(v.shape, lambda i, c: (0, 0)) for v in arrays],
            out_specs=(out_spec, out_spec),
        ),
        compiler_params=pltpu.CompilerParams(vmem_limit_bytes=40 * 1024 * 1024),
        cost_estimate=pl.CostEstimate(
            flops=2 * rows * depth * TILE * nb,
            bytes_accessed=rows * depth * 2 + nb * (depth + 2 * rows) * TILE * 2,
            transcendentals=0,
        ),
        name="tile_products",
    )(core, a, row_mask, *arrays)


def place_kernel(index_ref, s_ref, out_ref):
    slots = out_ref.shape[1] // ROWS
    for d in range(out_ref.shape[0]):
        for k in range(slots):
            t = index_ref[d * slots + k]
            value = s_ref[jnp.maximum(t, 0)]
            value = jnp.where(t >= 0, value, jnp.zeros_like(value))
            out_ref[d, k * ROWS : (k + 1) * ROWS, :] = value.astype(out_ref.dtype)


def place(index, s, peers):
    return pl.pallas_call(
        place_kernel,
        out_shape=jax.ShapeDtypeStruct((peers, CAP * ROWS, TILE), jnp.bfloat16),
        in_specs=[
            pl.BlockSpec(memory_space=pltpu.SMEM),
            pl.BlockSpec(memory_space=pltpu.VMEM),
        ],
        out_specs=pl.BlockSpec(memory_space=pltpu.VMEM),
        name="place_tiles",
    )(index, s)


def per_device(integrals, density, mask_int, mask_den, owner_map):
    depth = density.shape[0]
    half = depth // 2
    k_tiles = depth // TILE
    layer = lax.axis_index("layer")
    row = lax.axis_index("row")
    core = (layer % 2).reshape(1)

    own = (
        density.reshape(k_tiles, TILE, TILE) * mask_den.astype(jnp.bfloat16)[:, :, None]
    ).reshape(depth, TILE)
    row_mask = jnp.repeat(mask_int.astype(jnp.bfloat16), TILE, axis=1)[:, None, :]

    l0 = from_left(own)
    r0 = from_right(own)
    p0 = from_pair(own)
    l1a = from_left(p0[:half])
    l1b = from_pair(l0[half:])
    r1a = from_right(p0[:half])
    o0a = from_left(l0[:half])
    o0b = from_right(r0[half:])
    r1b = from_pair(r0[half:])
    c1, c2 = 5 * TILE, 27 * TILE
    o1p = from_pair(o0a[c1:])
    o1l = from_left(l1b[: c2 - half])
    o1r = from_right(jnp.concatenate([r1a[:c1], r1b[c2 - half :]], axis=0))

    whole = [(0, depth)]
    lo, hi = [(0, half)], [(half, depth)]
    groups = [
        [[(own, whole)], [(l0, whole)], [(r0, whole)], [(p0, whole)]],
        [[(l1a, lo), (l1b, hi)]],
        [[(r1a, lo), (r1b, hi)], [(o0a, lo), (o0b, hi)]],
        [[(o1p, [(c1, half)]), (o1l, [(half, c2)]), (o1r, [(0, c1), (c2, depth)])]],
    ]
    sums = []
    for blocks in groups:
        mine, other = matmul(core, integrals, row_mask, blocks)
        chip = mine + lax.ppermute(other, "layer", CORE_SWAP)
        part = jnp.sum(
            lax.all_to_all(chip, "col", split_axis=0, concat_axis=0, tiled=True), axis=0
        )
        total = part + lax.ppermute(part, "layer", YLO_SWAP)
        sums.append(total.reshape(-1, ROWS, TILE))
    s = jnp.concatenate(sums, axis=0)

    x, h = row // 2, row % 2
    order = [(0, 0), (-1, 0), (1, 0), (0, 1), (-1, 1), (1, 1), (2, 0), (2, 1)]
    cols = jnp.stack([2 * ((x + dx) % NX) + (h + dh) % 2 for dx, dh in order])
    count = owner_map.shape[1]
    owners = owner_map.reshape(count)
    number = jnp.arange(count, dtype=jnp.int32)
    earlier = (owners[None, :] == owners[:, None]) & (number[None, :] < number[:, None])
    slots = jnp.sum(earlier.astype(jnp.int32), axis=1)
    arrival = jnp.arange(count, dtype=jnp.int32)
    n_cols = len(order)
    tile_at = (arrival % (count // n_cols)) * n_cols + jnp.sum(
        jnp.where(
            (arrival[:, None] // (count // n_cols)) == jnp.arange(n_cols)[None, :], cols[None, :], 0
        ),
        axis=1,
    )
    peers = 2 * NZ
    wanted = (layer // 2) * peers + jnp.arange(peers * CAP, dtype=jnp.int32) // CAP
    slot_at = jnp.arange(peers * CAP, dtype=jnp.int32) % CAP
    hit = (owners[None, :] == wanted[:, None]) & (slots[None, :] == slot_at[:, None])
    tile_of = jnp.sum(jnp.where(hit, number[None, :] + 1, 0), axis=1) - 1
    index = jnp.sum(
        jnp.where(tile_at[None, :] == tile_of[:, None], arrival[None, :] + 1, 0), axis=1
    ) - 1

    outgoing = place(index.astype(jnp.int32), s, peers)
    groups_of = [list(range(peers)), list(range(peers, 2 * peers))]
    arrived = lax.all_to_all(
        outgoing, ("layer", "col"), split_axis=0, concat_axis=0, axis_index_groups=groups_of, tiled=True
    )
    placed = arrived.reshape(peers, CAP, ROWS, TILE).transpose(1, 0, 2, 3)
    return placed.reshape(1, 1, CAP, TILE, TILE)


def solution(mesh):
    placed = (
        P("row", ("layer", "col")),
        P(("layer", "col"), "row"),
        P("row", ("layer", "col")),
        P(("layer", "col"), "row"),
        P("row", None, None),
    )
    return jax.shard_map(
        per_device,
        mesh=mesh,
        in_specs=placed,
        out_specs=P("row", ("layer", "col"), None, None, None),
        check_vma=False,
    )
```

```python
import functools
import jax
import jax.numpy as jnp
from jax import lax
from jax.experimental import pallas as pl
from jax.experimental.pallas import tpu as pltpu
from jax.sharding import PartitionSpec as P

TILE = 128
CAP = 4
NX = 4
NZ = 8
ROWS = 8
STEP = 2
FIRST = 4
ORDER = [(0, 0), (-1, 0), (1, 0), (0, 1), (2, 0), (-1, 1), (1, 1), (2, 1)]


LONG = pl.CostEstimate(flops=10**11, bytes_accessed=10**8, transcendentals=0)
SHORT = pl.CostEstimate(flops=1000, bytes_accessed=1000, transcendentals=0)


def x_shift(step):
    return [(2 * x + h, 2 * ((x + step) % NX) + h) for x in range(NX) for h in range(2)]


Y_SWAP = [(2 * x + h, 2 * x + 1 - h) for x in range(NX) for h in range(2)]
CORE_SWAP = [(i, i ^ 1) for i in range(4)]
YLO_SWAP = [(i, i ^ 2) for i in range(4)]


def from_left(v):
    return lax.ppermute(v, "row", x_shift(1))


def from_right(v):
    return lax.ppermute(v, "row", x_shift(-1))


def from_pair(v):
    return lax.ppermute(v, "row", Y_SWAP)


def mask_rows(a, mask):
    rows, depth = a.shape
    by_row = jnp.repeat(mask.astype(jnp.bfloat16), TILE, axis=1)[:, None, :]

    def kernel(a_ref, m_ref, o_ref):
        o_ref[...] = a_ref[...] * m_ref[0]

    return pl.pallas_call(
        kernel,
        out_shape=pltpu.HBM(a.shape, a.dtype),
        grid=(rows // TILE,),
        in_specs=[
            pl.BlockSpec((TILE, depth), lambda i: (i, 0)),
            pl.BlockSpec((1, 1, depth), lambda i: (i, 0, 0)),
        ],
        out_specs=pl.BlockSpec((TILE, depth), lambda i: (i, 0)),
        compiler_params=pltpu.CompilerParams(vmem_limit_bytes=16 * 1024 * 1024),
        cost_estimate=SHORT,
        name="mask_integrals",
    )(a, by_row)


def matmul_kernel(nb, per_block, y_first, where_ref, a_hbm, *refs):
    n = nb * per_block
    pieces, (mine, other, left, sems) = refs[:n], refs[n:]
    first_core, y_lo = where_ref[0] == 0, where_ref[1]
    chunks, step, depth = left.shape
    tiles = step // TILE
    copies = [
        pltpu.make_async_copy(a_hbm.at[pl.ds(i * step, step), :], left.at[i], sems.at[i])
        for i in range(chunks)
    ]
    for copy in copies:
        copy.start()
    span = depth // per_block
    for i in range(chunks):
        copies[i].wait()
        for j in range(0, nb, 2):
            width = min(2, nb - j)
            acc = None
            for p in range(per_block):
                right = [pieces[per_block * (j + w) + p][...] for w in range(width)]
                right = right[0] if width == 1 else jnp.concatenate(right, axis=1)
                part = jnp.dot(
                    left[i, :, p * span : (p + 1) * span],
                    right,
                    preferred_element_type=jnp.float32,
                )
                acc = part if acc is None else acc + part
            for w in range(width):
                halves = acc[:, w * TILE : (w + 1) * TILE].reshape(tiles, 2, NZ, ROWS, TILE)
                for t in range(tiles):
                    kept = jnp.where(first_core, halves[t, 0], halves[t, 1])
                    sent = jnp.where(first_core, halves[t, 1], halves[t, 0])
                    at = i * tiles + t
                    if y_first:
                        per = chunks * tiles // 2
                        side = lax.bitwise_xor(y_lo, at // per)
                        mine[side, :, j + w, at % per] = kept
                        other[side, :, j + w, at % per] = sent
                    else:
                        mine[:, j + w, at] = kept
                        other[:, j + w, at] = sent


def matmul(where, a, blocks, y_first, cost):
    rows, depth = a.shape
    tiles = rows // TILE
    nb, per_block = len(blocks), len(blocks[0])
    step = STEP * TILE
    arrays = [v for b in blocks for v in b]
    if y_first:
        out = jax.ShapeDtypeStruct((2, NZ, nb, tiles // 2, ROWS, TILE), jnp.float32)
    else:
        out = jax.ShapeDtypeStruct((NZ, nb, tiles, ROWS, TILE), jnp.float32)
    in_vmem = pl.BlockSpec(memory_space=pltpu.VMEM)
    return pl.pallas_call(
        functools.partial(matmul_kernel, nb, per_block, y_first),
        out_shape=(out, out),
        in_specs=[pl.BlockSpec(memory_space=pltpu.SMEM), pl.BlockSpec(memory_space=pltpu.HBM)]
        + [in_vmem] * len(arrays),
        out_specs=(in_vmem, in_vmem),
        scratch_shapes=[
            pltpu.VMEM((rows // step, step, depth), a.dtype),
            pltpu.SemaphoreType.DMA((rows // step,)),
        ],
        compiler_params=pltpu.CompilerParams(vmem_limit_bytes=24 * 1024 * 1024),
        cost_estimate=cost,
        name="tile_products",
    )(where, a, *arrays)


def place_kernel(index_ref, own1, pair1, own2, pair2, out_ref, s):
    at = own1.shape[0]
    s[:at] = own1[...] + pair1[...]
    for part in (own2, pair2):
        s[at : at + part.shape[0]] = part[...]
        at += part.shape[0]
    for d in range(out_ref.shape[0]):
        for k in range(0, CAP, 2):
            both = []
            for w in range(2):
                t = index_ref[d * CAP + k + w]
                value = s[jnp.maximum(t, 0)]
                both.append(jnp.where(t >= 0, value, jnp.zeros_like(value)))
            out_ref[d, k * ROWS : (k + 2) * ROWS, :] = jnp.concatenate(both, axis=0).astype(
                out_ref.dtype
            )


def place(index, parts, peers):
    held = sum(v.shape[0] for v in parts[0::2]) + parts[-1].shape[0]
    return pl.pallas_call(
        place_kernel,
        out_shape=jax.ShapeDtypeStruct((peers, CAP * ROWS, TILE), jnp.bfloat16),
        in_specs=[pl.BlockSpec(memory_space=pltpu.SMEM)]
        + [pl.BlockSpec(memory_space=pltpu.VMEM)] * len(parts),
        out_specs=pl.BlockSpec(memory_space=pltpu.VMEM),
        scratch_shapes=[pltpu.VMEM((held, ROWS, TILE), jnp.float32)],
        name="place_tiles",
    )(index, *parts)


def placement(owner_map, row, y_lo, peers):
    count = owner_map.shape[1]
    owners = owner_map.reshape(count)
    number = jnp.arange(count, dtype=jnp.int32)
    earlier = (owners[None, :] == owners[:, None]) & (number[None, :] < number[:, None])
    slots = jnp.sum(earlier.astype(jnp.int32), axis=1)
    n_cols = len(ORDER)
    a, b = number // n_cols, number % n_cols
    n_rows = count // n_cols
    half = n_rows // 2
    summed = FIRST * n_rows
    arrival = jnp.zeros_like(number)
    for j, (dx, dh) in enumerate(ORDER):
        col = 2 * ((row // 2 + dx + NX) % NX) + (row + dh) % 2
        if j < FIRST:
            at = j * n_rows + a
        else:
            late = jnp.where(a // half == y_lo, 0, (n_cols - FIRST) * half)
            at = summed + late + (j - FIRST) * half + a % half
        arrival = arrival + jnp.where(b == col, at, 0)
    wanted = y_lo * peers * CAP + jnp.arange(peers * CAP, dtype=jnp.int32)
    hit = (owners[None, :] * CAP + slots[None, :]) == wanted[:, None]
    return jnp.sum(jnp.where(hit, arrival[None, :] + 1, 0), axis=1).astype(jnp.int32) - 1


def per_device(integrals, density, mask_int, mask_den, owner_map):
    depth = density.shape[0]
    half = depth // 2
    k_tiles = depth // TILE
    layer = lax.axis_index("layer")
    row = lax.axis_index("row")
    y_lo = layer // 2
    where = jnp.stack([layer % 2, y_lo]).astype(jnp.int32)
    hold = lax.optimization_barrier

    scale = mask_den.astype(jnp.bfloat16)[:, :, None]
    own = (density.reshape(k_tiles, TILE, TILE) * scale).reshape(depth, TILE)

    def products(blocks, y_first, cost):
        return matmul(where, masked, blocks, y_first, cost)

    def of_chip(parts):
        mine, other = parts
        return mine + lax.ppermute(other, "layer", CORE_SWAP)

    def to_z(chip):
        return lax.all_to_all(chip, "col", split_axis=0, concat_axis=0, tiled=True)

    def shared(came):
        share = jnp.sum(came, axis=0).reshape(-1, ROWS, TILE)
        return share, lax.ppermute(share, "layer", YLO_SWAP)

    def of_y(chip):
        return chip[0] + lax.ppermute(chip[1], "layer", YLO_SWAP)

    l0, r0, p0 = from_left(own), from_right(own), from_pair(own)
    masked = mask_rows(integrals, mask_int)
    l0, r0, p0, masked = hold((l0, r0, p0, masked))
    r0b = r0[half:]
    o0a, o0b, r1b = from_left(l0[:half]), from_right(r0b), from_pair(r0b)
    prod1 = products([(own,), (l0,), (r0,), (p0,)], False, LONG)
    o0a, o0b, r1b, l0, p0, prod1 = hold((o0a, o0b, r1b, l0, p0, prod1))
    p0a = p0[:half]
    l1a, r1a, l1b = from_left(p0a), from_right(p0a), from_pair(l0[half:])
    o1a, o1b = from_pair(o0a), from_right(r1b)
    chip1 = of_chip(prod1)
    came1 = to_z(chip1)
    l1a, l1b, r1a, chip1 = hold((l1a, l1b, r1a, chip1))
    prod2 = products([(o0a, o0b), (l1a, l1b)], True, LONG)
    o1a, o1b, prod2 = hold((o1a, o1b, prod2))
    prod3 = products([(r1a, r1b), (o1a, o1b)], True, SHORT)
    prod3, both2, came1 = hold((prod3, of_y(of_chip(prod2)), came1))
    came2 = to_z(jnp.concatenate([both2, of_y(of_chip(prod3))], axis=1))

    parts = shared(came1) + shared(came2)
    peers = 2 * NZ
    outgoing = place(placement(owner_map, row, y_lo, peers), parts, peers)
    arrived = lax.all_to_all(
        outgoing,
        ("layer", "col"),
        split_axis=0,
        concat_axis=0,
        axis_index_groups=[list(range(peers)), list(range(peers, 2 * peers))],
        tiled=True,
    )
    placed = arrived.reshape(peers, CAP, ROWS, TILE).transpose(1, 0, 2, 3)
    return placed.reshape(1, 1, CAP, TILE, TILE)


def solution(mesh):
    placed = (
        P("row", ("layer", "col")),
        P(("layer", "col"), "row"),
        P("row", ("layer", "col")),
        P(("layer", "col"), "row"),
        P("row", None, None),
    )
    return jax.shard_map(
        per_device,
        mesh=mesh,
        in_specs=placed,
        out_specs=P("row", ("layer", "col"), None, None, None),
        check_vma=False,
    )
```

```python
import functools
import jax
import jax.numpy as jnp
from jax import lax
from jax.experimental import pallas as pl
from jax.experimental.pallas import tpu as pltpu
from jax.sharding import PartitionSpec as P

TILE = 128
CAP = 4
NX = 4
NZ = 8
ROWS = 8
STEP = 2
ORDER = [(0, 0), (-1, 0), (1, 0), (0, 1), (2, 0), (-1, 1), (1, 1), (2, 1)]


LONG = pl.CostEstimate(flops=10**11, bytes_accessed=10**8, transcendentals=0)
SHORT = pl.CostEstimate(flops=1000, bytes_accessed=1000, transcendentals=0)


def x_shift(step):
    return [(2 * x + h, 2 * ((x + step) % NX) + h) for x in range(NX) for h in range(2)]


Y_SWAP = [(2 * x + h, 2 * x + 1 - h) for x in range(NX) for h in range(2)]
CORE_SWAP = [(i, i ^ 1) for i in range(4)]
YLO_SWAP = [(i, i ^ 2) for i in range(4)]


def from_left(v):
    return lax.ppermute(v, "row", x_shift(1))


def from_right(v):
    return lax.ppermute(v, "row", x_shift(-1))


def from_pair(v):
    return lax.ppermute(v, "row", Y_SWAP)


def small_call(kernel, out_shape, name, limit=8):
    return pl.pallas_call(
        kernel,
        out_shape=out_shape,
        compiler_params=pltpu.CompilerParams(vmem_limit_bytes=limit * 1024 * 1024),
        cost_estimate=SHORT,
        name=name,
    )


def mask_rows(a, mask):
    rows, depth = a.shape
    by_row = jnp.repeat(mask.astype(jnp.bfloat16), TILE, axis=1)[:, None, :]

    def kernel(a_ref, m_ref, o_ref):
        at = pl.multiple_of(pl.program_id(0) * TILE, TILE)
        o_ref[pl.ds(at, TILE), :] = a_ref[...] * m_ref[0]

    return pl.pallas_call(
        kernel,
        out_shape=pltpu.VMEM(a.shape, a.dtype),
        grid=(rows // TILE,),
        in_specs=[
            pl.BlockSpec((TILE, depth), lambda i: (i, 0)),
            pl.BlockSpec((1, 1, depth), lambda i: (i, 0, 0)),
        ],
        out_specs=pl.BlockSpec(memory_space=pltpu.VMEM),
        compiler_params=pltpu.CompilerParams(vmem_limit_bytes=16 * 1024 * 1024),
        cost_estimate=SHORT,
        name="mask_integrals",
    )(a, by_row)


def split(l0, r0, p0):
    half = l0.shape[0] // 2

    def kernel(l_ref, r_ref, p_ref, la, lb, rb, pa):
        la[...] = l_ref[:half, :]
        lb[...] = l_ref[half:, :]
        rb[...] = r_ref[half:, :]
        pa[...] = p_ref[:half, :]

    out = jax.ShapeDtypeStruct((half, l0.shape[1]), l0.dtype)
    return small_call(kernel, (out,) * 4, "split_blocks")(l0, r0, p0)


def add(a, b):
    def kernel(a_ref, b_ref, o_ref):
        o_ref[...] = a_ref[...] + b_ref[...]

    return small_call(kernel, jax.ShapeDtypeStruct(a.shape, a.dtype), "add_cores")(a, b)


def add_for_z(z, a0, b0, a1, b1):
    def kernel(z_ref, a0_ref, b0_ref, a1_ref, b1_ref, *outs):
        n = a0_ref.shape[1]
        for d, o_ref in enumerate(outs):
            to = lax.rem(z_ref[0] + d, NZ)
            o_ref[:n] = a0_ref[to] + b0_ref[to]
            o_ref[n:] = a1_ref[to] + b1_ref[to]

    out = jax.ShapeDtypeStruct((a0.shape[1] + a1.shape[1], ROWS, TILE), a0.dtype)
    in_vmem = pl.BlockSpec(memory_space=pltpu.VMEM)
    return pl.pallas_call(
        kernel,
        out_shape=(out,) * NZ,
        in_specs=[pl.BlockSpec(memory_space=pltpu.SMEM)] + [in_vmem] * 4,
        out_specs=(in_vmem,) * NZ,
        compiler_params=pltpu.CompilerParams(vmem_limit_bytes=16 * 1024 * 1024),
        cost_estimate=SHORT,
        name="add_for_z",
    )(z, a0, b0, a1, b1)


def add_pairs(*pairs):
    def kernel(*refs):
        n = len(pairs)
        for i in range(n):
            refs[2 * n + i][...] = refs[2 * i][...] + refs[2 * i + 1][...]

    out = tuple(jax.ShapeDtypeStruct(p[0].shape, p[0].dtype) for p in pairs)
    return small_call(kernel, out, "add_pairs")(*[v for p in pairs for v in p])


def add_three(a, b, c):
    def kernel(a_ref, b_ref, c_ref, o_ref):
        o_ref[...] = a_ref[...] + b_ref[...] + c_ref[...]

    return small_call(kernel, jax.ShapeDtypeStruct(a.shape, a.dtype), "add_three")(a, b, c)


def matmul_kernel(nb, per_block, core_ref, a_ref, *refs):
    n = nb * per_block
    pieces, (mine, other) = refs[:n], refs[n:]
    first_core = core_ref[0] == 0
    rows, depth = a_ref.shape
    step = STEP * TILE
    span = depth // per_block
    for i in range(rows // step):
        for j in range(0, nb, 2):
            width = min(2, nb - j)
            acc = None
            for p in range(per_block):
                right = [pieces[per_block * (j + w) + p][...] for w in range(width)]
                right = right[0] if width == 1 else jnp.concatenate(right, axis=1)
                part = jnp.dot(
                    a_ref[i * step : (i + 1) * step, p * span : (p + 1) * span],
                    right,
                    preferred_element_type=jnp.float32,
                )
                acc = part if acc is None else acc + part
            for w in range(width):
                halves = acc[:, w * TILE : (w + 1) * TILE].reshape(STEP, 2, NZ, ROWS, TILE)
                for t in range(STEP):
                    kept = jnp.where(first_core, halves[t, 0], halves[t, 1])
                    sent = jnp.where(first_core, halves[t, 1], halves[t, 0])
                    at = i * STEP + t
                    mine[:, j + w, at] = kept
                    other[:, j + w, at] = sent


def matmul(core, a, blocks, cost):
    tiles = a.shape[0] // TILE
    nb, per_block = len(blocks), len(blocks[0])
    arrays = [v for b in blocks for v in b]
    out = jax.ShapeDtypeStruct((NZ, nb, tiles, ROWS, TILE), jnp.float32)
    in_vmem = pl.BlockSpec(memory_space=pltpu.VMEM)
    return pl.pallas_call(
        functools.partial(matmul_kernel, nb, per_block),
        out_shape=(out, out),
        in_specs=[pl.BlockSpec(memory_space=pltpu.SMEM)] + [in_vmem] * (1 + len(arrays)),
        out_specs=(in_vmem, in_vmem),
        compiler_params=pltpu.CompilerParams(vmem_limit_bytes=18 * 1024 * 1024),
        cost_estimate=cost,
        name="tile_products",
    )(core, a, *arrays)


def place_kernel(index_ref, own1, pair1, own2, pair2, out_ref, s):
    at = own1.shape[0]
    s[:at] = own1[...] + pair1[...]
    s[at:] = own2[...] + pair2[...]
    for d in range(out_ref.shape[0]):
        for k in range(0, CAP, 2):
            both = []
            for w in range(2):
                t = index_ref[d * CAP + k + w]
                value = s[jnp.maximum(t, 0)]
                both.append(jnp.where(t >= 0, value, jnp.zeros_like(value)))
            out_ref[d, k * ROWS : (k + 2) * ROWS, :] = jnp.concatenate(both, axis=0).astype(
                out_ref.dtype
            )


def place(index, parts, peers):
    held = parts[0].shape[0] + parts[2].shape[0]
    return pl.pallas_call(
        place_kernel,
        out_shape=jax.ShapeDtypeStruct((peers, CAP * ROWS, TILE), jnp.bfloat16),
        in_specs=[pl.BlockSpec(memory_space=pltpu.SMEM)]
        + [pl.BlockSpec(memory_space=pltpu.VMEM)] * len(parts),
        out_specs=pl.BlockSpec(memory_space=pltpu.VMEM),
        scratch_shapes=[pltpu.VMEM((held, ROWS, TILE), jnp.float32)],
        compiler_params=pltpu.CompilerParams(vmem_limit_bytes=8 * 1024 * 1024),
        name="place_tiles",
    )(index, *parts)


def placement(owner_map, row, y_lo, peers):
    count = owner_map.shape[1]
    owners = owner_map.reshape(count)
    number = jnp.arange(count, dtype=jnp.int32)
    earlier = (owners[None, :] == owners[:, None]) & (number[None, :] < number[:, None])
    slots = jnp.sum(earlier.astype(jnp.int32), axis=1)
    n_cols = len(ORDER)
    a, b = number // n_cols, number % n_cols
    n_rows = count // n_cols
    arrival = jnp.zeros_like(number)
    for j, (dx, dh) in enumerate(ORDER):
        col = 2 * ((row // 2 + dx + NX) % NX) + (row + dh) % 2
        arrival = arrival + jnp.where(b == col, j * n_rows + a, 0)
    wanted = y_lo * peers * CAP + jnp.arange(peers * CAP, dtype=jnp.int32)
    hit = (owners[None, :] * CAP + slots[None, :]) == wanted[:, None]
    return jnp.sum(jnp.where(hit, arrival[None, :] + 1, 0), axis=1).astype(jnp.int32) - 1


def per_device(integrals, density, mask_int, mask_den, owner_map):
    depth = density.shape[0]
    half = depth // 2
    k_tiles = depth // TILE
    layer = lax.axis_index("layer")
    row = lax.axis_index("row")
    y_lo = layer // 2
    z = lax.axis_index("col").astype(jnp.int32).reshape(1)
    core = (layer % 2).astype(jnp.int32).reshape(1)
    hold = lax.optimization_barrier

    scale = mask_den.astype(jnp.bfloat16)[:, :, None]
    own = (density.reshape(k_tiles, TILE, TILE) * scale).reshape(depth, TILE)

    def products(blocks, cost):
        return matmul(core, masked, blocks, cost)

    def core_swap(v):
        return lax.ppermute(v, "layer", CORE_SWAP)

    def y_swap(v):
        return lax.ppermute(v, "layer", YLO_SWAP)

    def to_z(chip):
        return lax.all_to_all(chip, "col", split_axis=0, concat_axis=0, tiled=True)

    def z_shift(v, step):
        return lax.ppermute(v, "col", [(i, (i + step) % NZ) for i in range(NZ)])

    def tiles(v):
        return v.reshape(NZ, -1, ROWS, TILE)

    l0, r0, p0 = from_left(own), from_right(own), from_pair(own)
    integrals, core, z = hold((integrals, core, z))
    masked = mask_rows(integrals, mask_int)
    l0, r0, p0, masked = hold((l0, r0, p0, masked))
    l0a, l0b, r0b, p0a = split(l0, r0, p0)
    o0a, o0b, r1b = from_left(l0a), from_right(r0b), from_pair(r0b)
    mine1, other1 = products([(own,), (l0,), (r0,), (p0,)], LONG)
    o0a, o0b, r1b, l0b, p0a, mine1, other1 = hold((o0a, o0b, r1b, l0b, p0a, mine1, other1))
    l1a, r1a, l1b = from_left(p0a), from_right(p0a), from_pair(l0b)
    o1a, o1b = from_pair(o0a), from_right(r1b)
    chip1 = add(mine1, core_swap(other1))
    came1 = to_z(chip1)
    l1a, l1b, r1a, chip1 = hold((l1a, l1b, r1a, chip1))
    mine2, other2 = products([(o0a, o0b), (l1a, l1b)], LONG)
    o1a, o1b, mine2, other2 = hold((o1a, o1b, mine2, other2))
    mine3, other3 = products([(r1a, r1b), (o1a, o1b)], SHORT)
    by_z = add_for_z(
        z, tiles(mine2), tiles(core_swap(other2)), tiles(mine3), tiles(core_swap(other3))
    )
    owner_map, *by_z = hold((owner_map, *by_z))
    down, up = z_shift(by_z[4], -1), z_shift(by_z[3], 1)
    down, up = add_pairs((down, by_z[5]), (up, by_z[2]))
    down, up = z_shift(down, -1), z_shift(up, 1)
    down, up, came1 = hold((*add_pairs((down, by_z[6]), (up, by_z[1])), came1))
    down, up = z_shift(down, -1), z_shift(up, 1)
    share1 = jnp.sum(came1, axis=0).reshape(-1, ROWS, TILE)
    pair1 = y_swap(share1)
    down, share1 = hold((down, share1))
    (down,) = add_pairs((down, by_z[7]))
    down = z_shift(down, -1)
    down, up, pair1 = hold((down, up, pair1))
    share2 = add_three(by_z[0], down, up)

    parts = share1, pair1, share2, y_swap(share2)
    peers = 2 * NZ
    outgoing = place(placement(owner_map, row, y_lo, peers), parts, peers)
    arrived = lax.all_to_all(
        outgoing,
        ("layer", "col"),
        split_axis=0,
        concat_axis=0,
        axis_index_groups=[list(range(peers)), list(range(peers, 2 * peers))],
        tiled=True,
    )
    placed = arrived.reshape(peers, CAP, ROWS, TILE).transpose(1, 0, 2, 3)
    return placed.reshape(1, 1, CAP, TILE, TILE)


def solution(mesh):
    placed = (
        P("row", ("layer", "col")),
        P(("layer", "col"), "row"),
        P("row", ("layer", "col")),
        P(("layer", "col"), "row"),
        P("row", None, None),
    )
    return jax.shard_map(
        per_device,
        mesh=mesh,
        in_specs=placed,
        out_specs=P("row", ("layer", "col"), None, None, None),
        check_vma=False,
    )
```

```python
import functools
import jax
import jax.numpy as jnp
from jax import lax
from jax.experimental import pallas as pl
from jax.experimental.pallas import tpu as pltpu
from jax.sharding import PartitionSpec as P

TILE = 128
CAP = 4
NX = 4
NZ = 8
ROWS = 8
STEP = 2
ORDER = [(0, 0), (-1, 0), (1, 0), (0, 1), (2, 0), (-1, 1), (1, 1), (2, 1)]


LONG = pl.CostEstimate(flops=10**11, bytes_accessed=10**8, transcendentals=0)
SHORT = pl.CostEstimate(flops=1000, bytes_accessed=1000, transcendentals=0)


def x_shift(step):
    return [(2 * x + h, 2 * ((x + step) % NX) + h) for x in range(NX) for h in range(2)]


Y_SWAP = [(2 * x + h, 2 * x + 1 - h) for x in range(NX) for h in range(2)]
CORE_SWAP = [(i, i ^ 1) for i in range(4)]
YLO_SWAP = [(i, i ^ 2) for i in range(4)]


def from_left(v):
    return lax.ppermute(v, "row", x_shift(1))


def from_right(v):
    return lax.ppermute(v, "row", x_shift(-1))


def from_pair(v):
    return lax.ppermute(v, "row", Y_SWAP)


def small_call(kernel, out_shape, name, limit=8):
    return pl.pallas_call(
        kernel,
        out_shape=out_shape,
        compiler_params=pltpu.CompilerParams(vmem_limit_bytes=limit * 1024 * 1024),
        cost_estimate=SHORT,
        name=name,
    )


def mask_rows(a, mask):
    rows, depth = a.shape
    by_row = jnp.repeat(mask.astype(jnp.bfloat16), TILE, axis=1)[:, None, :]

    def kernel(a_ref, m_ref, o_ref):
        at = pl.multiple_of(pl.program_id(0) * TILE, TILE)
        o_ref[pl.ds(at, TILE), :] = a_ref[...] * m_ref[0]

    return pl.pallas_call(
        kernel,
        out_shape=pltpu.VMEM(a.shape, a.dtype),
        grid=(rows // TILE,),
        in_specs=[
            pl.BlockSpec((TILE, depth), lambda i: (i, 0)),
            pl.BlockSpec((1, 1, depth), lambda i: (i, 0, 0)),
        ],
        out_specs=pl.BlockSpec(memory_space=pltpu.VMEM),
        compiler_params=pltpu.CompilerParams(vmem_limit_bytes=16 * 1024 * 1024),
        cost_estimate=SHORT,
        name="mask_integrals",
    )(a, by_row)


def split(l0, r0, p0):
    half = l0.shape[0] // 2

    def kernel(l_ref, r_ref, p_ref, la, lb, rb, pa):
        la[...] = l_ref[:half, :]
        lb[...] = l_ref[half:, :]
        rb[...] = r_ref[half:, :]
        pa[...] = p_ref[:half, :]

    out = jax.ShapeDtypeStruct((half, l0.shape[1]), l0.dtype)
    return small_call(kernel, (out,) * 4, "split_blocks")(l0, r0, p0)


def add(a, b):
    def kernel(a_ref, b_ref, o_ref):
        o_ref[...] = a_ref[...] + b_ref[...]

    return small_call(kernel, jax.ShapeDtypeStruct(a.shape, a.dtype), "add_cores")(a, b)


def add_for_z(z, a0, b0, a1, b1):
    def kernel(z_ref, a0_ref, b0_ref, a1_ref, b1_ref, *outs):
        n = a0_ref.shape[1]
        for d, o_ref in enumerate(outs):
            to = lax.rem(z_ref[0] + d, NZ)
            o_ref[:n] = a0_ref[to] + b0_ref[to]
            o_ref[n:] = a1_ref[to] + b1_ref[to]

    out = jax.ShapeDtypeStruct((a0.shape[1] + a1.shape[1], ROWS, TILE), a0.dtype)
    in_vmem = pl.BlockSpec(memory_space=pltpu.VMEM)
    return pl.pallas_call(
        kernel,
        out_shape=(out,) * NZ,
        in_specs=[pl.BlockSpec(memory_space=pltpu.SMEM)] + [in_vmem] * 4,
        out_specs=(in_vmem,) * NZ,
        compiler_params=pltpu.CompilerParams(vmem_limit_bytes=16 * 1024 * 1024),
        cost_estimate=SHORT,
        name="add_for_z",
    )(z, a0, b0, a1, b1)


def add_pairs(*pairs):
    def kernel(*refs):
        n = len(pairs)
        for i in range(n):
            refs[2 * n + i][...] = refs[2 * i][...] + refs[2 * i + 1][...]

    out = tuple(jax.ShapeDtypeStruct(p[0].shape, p[0].dtype) for p in pairs)
    return small_call(kernel, out, "add_pairs")(*[v for p in pairs for v in p])


def matmul_kernel(nb, per_block, core_ref, a_ref, *refs):
    n = nb * per_block
    pieces, (mine, other) = refs[:n], refs[n:]
    first_core = core_ref[0] == 0
    rows, depth = a_ref.shape
    step = STEP * TILE
    span = depth // per_block
    for i in range(rows // step):
        for j in range(0, nb, 2):
            width = min(2, nb - j)
            acc = None
            for p in range(per_block):
                right = [pieces[per_block * (j + w) + p][...] for w in range(width)]
                right = right[0] if width == 1 else jnp.concatenate(right, axis=1)
                part = jnp.dot(
                    a_ref[i * step : (i + 1) * step, p * span : (p + 1) * span],
                    right,
                    preferred_element_type=jnp.float32,
                )
                acc = part if acc is None else acc + part
            for w in range(width):
                halves = acc[:, w * TILE : (w + 1) * TILE].reshape(STEP, 2, NZ, ROWS, TILE)
                for t in range(STEP):
                    kept = jnp.where(first_core, halves[t, 0], halves[t, 1])
                    sent = jnp.where(first_core, halves[t, 1], halves[t, 0])
                    at = i * STEP + t
                    mine[:, j + w, at] = kept
                    other[:, j + w, at] = sent


def matmul(core, a, blocks, cost):
    tiles = a.shape[0] // TILE
    nb, per_block = len(blocks), len(blocks[0])
    arrays = [v for b in blocks for v in b]
    out = jax.ShapeDtypeStruct((NZ, nb, tiles, ROWS, TILE), jnp.float32)
    in_vmem = pl.BlockSpec(memory_space=pltpu.VMEM)
    return pl.pallas_call(
        functools.partial(matmul_kernel, nb, per_block),
        out_shape=(out, out),
        in_specs=[pl.BlockSpec(memory_space=pltpu.SMEM)] + [in_vmem] * (1 + len(arrays)),
        out_specs=(in_vmem, in_vmem),
        compiler_params=pltpu.CompilerParams(vmem_limit_bytes=18 * 1024 * 1024),
        cost_estimate=cost,
        name="tile_products",
    )(core, a, *arrays)


def place_kernel(index_ref, own1, pair1, own2, pair2, last, cross, out_ref, s):
    at = own1.shape[0]
    s[:at] = own1[...] + pair1[...]
    s[at:] = (own2[...] + last[...]) + (pair2[...] + cross[...])
    for d in range(out_ref.shape[0]):
        for k in range(0, CAP, 2):
            both = []
            for w in range(2):
                t = index_ref[d * CAP + k + w]
                value = s[jnp.maximum(t, 0)]
                both.append(jnp.where(t >= 0, value, jnp.zeros_like(value)))
            out_ref[d, k * ROWS : (k + 2) * ROWS, :] = jnp.concatenate(both, axis=0).astype(
                out_ref.dtype
            )


def place(index, parts, peers):
    held = parts[0].shape[0] + parts[2].shape[0]
    return pl.pallas_call(
        place_kernel,
        out_shape=jax.ShapeDtypeStruct((peers, CAP * ROWS, TILE), jnp.bfloat16),
        in_specs=[pl.BlockSpec(memory_space=pltpu.SMEM)]
        + [pl.BlockSpec(memory_space=pltpu.VMEM)] * len(parts),
        out_specs=pl.BlockSpec(memory_space=pltpu.VMEM),
        scratch_shapes=[pltpu.VMEM((held, ROWS, TILE), jnp.float32)],
        compiler_params=pltpu.CompilerParams(vmem_limit_bytes=8 * 1024 * 1024),
        name="place_tiles",
    )(index, *parts)


def placement(owner_map, row, y_lo, peers):
    count = owner_map.shape[1]
    owners = owner_map.reshape(count)
    number = jnp.arange(count, dtype=jnp.int32)
    earlier = (owners[None, :] == owners[:, None]) & (number[None, :] < number[:, None])
    slots = jnp.sum(earlier.astype(jnp.int32), axis=1)
    n_cols = len(ORDER)
    a, b = number // n_cols, number % n_cols
    n_rows = count // n_cols
    arrival = jnp.zeros_like(number)
    for j, (dx, dh) in enumerate(ORDER):
        col = 2 * ((row // 2 + dx + NX) % NX) + (row + dh) % 2
        arrival = arrival + jnp.where(b == col, j * n_rows + a, 0)
    wanted = y_lo * peers * CAP + jnp.arange(peers * CAP, dtype=jnp.int32)
    hit = (owners[None, :] * CAP + slots[None, :]) == wanted[:, None]
    return jnp.sum(jnp.where(hit, arrival[None, :] + 1, 0), axis=1).astype(jnp.int32) - 1


def per_device(integrals, density, mask_int, mask_den, owner_map):
    depth = density.shape[0]
    half = depth // 2
    k_tiles = depth // TILE
    layer = lax.axis_index("layer")
    row = lax.axis_index("row")
    y_lo = layer // 2
    z = lax.axis_index("col").astype(jnp.int32).reshape(1)
    core = (layer % 2).astype(jnp.int32).reshape(1)
    hold = lax.optimization_barrier

    scale = mask_den.astype(jnp.bfloat16)[:, :, None]
    own = (density.reshape(k_tiles, TILE, TILE) * scale).reshape(depth, TILE)

    def products(blocks, cost):
        return matmul(core, masked, blocks, cost)

    def core_swap(v):
        return lax.ppermute(v, "layer", CORE_SWAP)

    def y_swap(v):
        return lax.ppermute(v, "layer", YLO_SWAP)

    def to_z(chip):
        return lax.all_to_all(chip, "col", split_axis=0, concat_axis=0, tiled=True)

    def z_shift(v, step):
        return lax.ppermute(v, "col", [(i, (i + step) % NZ) for i in range(NZ)])

    def tiles(v):
        return v.reshape(NZ, -1, ROWS, TILE)

    l0, r0, p0 = from_left(own), from_right(own), from_pair(own)
    integrals, core, z = hold((integrals, core, z))
    masked = mask_rows(integrals, mask_int)
    l0, r0, p0, masked = hold((l0, r0, p0, masked))
    l0a, l0b, r0b, p0a = split(l0, r0, p0)
    o0a, o0b, r1b = from_left(l0a), from_right(r0b), from_pair(r0b)
    mine1, other1 = products([(own,), (l0,), (r0,), (p0,)], LONG)
    o0a, o0b, r1b, l0b, p0a, mine1, other1 = hold((o0a, o0b, r1b, l0b, p0a, mine1, other1))
    l1a, r1a, l1b = from_left(p0a), from_right(p0a), from_pair(l0b)
    o1a, o1b = from_pair(o0a), from_right(r1b)
    chip1 = add(mine1, core_swap(other1))
    came1 = to_z(chip1)
    l1a, l1b, r1a, chip1 = hold((l1a, l1b, r1a, chip1))
    mine2, other2 = products([(o0a, o0b), (l1a, l1b)], LONG)
    o1a, o1b, mine2, other2 = hold((o1a, o1b, mine2, other2))
    mine3, other3 = products([(r1a, r1b), (o1a, o1b)], SHORT)
    by_z = add_for_z(
        z, tiles(mine2), tiles(core_swap(other2)), tiles(mine3), tiles(core_swap(other3))
    )
    owner_map, *by_z = hold((owner_map, *by_z))
    down, up = z_shift(by_z[4], -1), z_shift(by_z[3], 1)
    down, up = add_pairs((down, by_z[5]), (up, by_z[2]))
    down, up = z_shift(down, -1), z_shift(up, 1)
    down, up, came1 = hold((*add_pairs((down, by_z[6]), (up, by_z[1])), came1))
    down, up = z_shift(down, -1), z_shift(up, 1)
    share1 = jnp.sum(came1, axis=0).reshape(-1, ROWS, TILE)
    pair1 = y_swap(share1)
    down, share1 = hold((down, share1))
    (down,) = add_pairs((down, by_z[7]))
    over = [
        (i * NZ + k, (i ^ 2) * NZ + (k - 1) % NZ) for i in range(len(CORE_SWAP)) for k in range(NZ)
    ]
    last, cross = z_shift(down, -1), lax.ppermute(down, ("layer", "col"), over)
    rest = add(by_z[0], up)
    parts = share1, pair1, rest, y_swap(rest), last, cross

    peers = 2 * NZ
    outgoing = place(placement(owner_map, row, y_lo, peers), parts, peers)
    arrived = lax.all_to_all(
        outgoing,
        ("layer", "col"),
        split_axis=0,
        concat_axis=0,
        axis_index_groups=[list(range(peers)), list(range(peers, 2 * peers))],
        tiled=True,
    )
    placed = arrived.reshape(peers, CAP, ROWS, TILE).transpose(1, 0, 2, 3)
    return placed.reshape(1, 1, CAP, TILE, TILE)


def solution(mesh):
    placed = (
        P("row", ("layer", "col")),
        P(("layer", "col"), "row"),
        P("row", ("layer", "col")),
        P(("layer", "col"), "row"),
        P("row", None, None),
    )
    return jax.shard_map(
        per_device,
        mesh=mesh,
        in_specs=placed,
        out_specs=P("row", ("layer", "col"), None, None, None),
        check_vma=False,
    )
```

```python
import functools
import jax
import jax.numpy as jnp
from jax import lax
from jax.experimental import pallas as pl
from jax.experimental.pallas import tpu as pltpu
from jax.sharding import PartitionSpec as P

TILE = 128
CAP = 4
NX = 4
NZ = 8
ROWS = 8
STEP = 2
ORDER = [(-1, 0), (1, 0), (0, 1), (2, 0), (-1, 1), (1, 1), (2, 1), (0, 0)]


LONG = pl.CostEstimate(flops=10**11, bytes_accessed=10**8, transcendentals=0)
SHORT = pl.CostEstimate(flops=1000, bytes_accessed=1000, transcendentals=0)


def x_shift(step):
    return [(2 * x + h, 2 * ((x + step) % NX) + h) for x in range(NX) for h in range(2)]


Y_SWAP = [(2 * x + h, 2 * x + 1 - h) for x in range(NX) for h in range(2)]
CORE_SWAP = [(i, i ^ 1) for i in range(4)]
YLO_SWAP = [(i, i ^ 2) for i in range(4)]


def from_left(v):
    return lax.ppermute(v, "row", x_shift(1))


def from_right(v):
    return lax.ppermute(v, "row", x_shift(-1))


def from_pair(v):
    return lax.ppermute(v, "row", Y_SWAP)


def small_call(kernel, out_shape, name, limit=8):
    return pl.pallas_call(
        kernel,
        out_shape=out_shape,
        compiler_params=pltpu.CompilerParams(vmem_limit_bytes=limit * 1024 * 1024),
        cost_estimate=SHORT,
        name=name,
    )


def mask_rows(a, mask):
    rows, depth = a.shape
    by_row = jnp.repeat(mask.astype(jnp.bfloat16), TILE, axis=1)[:, None, :]

    def kernel(a_ref, m_ref, o_ref):
        at = pl.multiple_of(pl.program_id(0) * TILE, TILE)
        o_ref[pl.ds(at, TILE), :] = a_ref[...] * m_ref[0]

    return pl.pallas_call(
        kernel,
        out_shape=pltpu.VMEM(a.shape, a.dtype),
        grid=(rows // TILE,),
        in_specs=[
            pl.BlockSpec((TILE, depth), lambda i: (i, 0)),
            pl.BlockSpec((1, 1, depth), lambda i: (i, 0, 0)),
        ],
        out_specs=pl.BlockSpec(memory_space=pltpu.VMEM),
        compiler_params=pltpu.CompilerParams(vmem_limit_bytes=16 * 1024 * 1024),
        cost_estimate=SHORT,
        name="mask_integrals",
    )(a, by_row)


def split(l0, r0, p0):
    half = l0.shape[0] // 2

    def kernel(l_ref, r_ref, p_ref, la, lb, rb, pa):
        la[...] = l_ref[:half, :]
        lb[...] = l_ref[half:, :]
        rb[...] = r_ref[half:, :]
        pa[...] = p_ref[:half, :]

    out = jax.ShapeDtypeStruct((half, l0.shape[1]), l0.dtype)
    return small_call(kernel, (out,) * 4, "split_blocks")(l0, r0, p0)


def add(a, b):
    def kernel(a_ref, b_ref, o_ref):
        o_ref[...] = a_ref[...] + b_ref[...]

    return small_call(kernel, jax.ShapeDtypeStruct(a.shape, a.dtype), "add_cores")(a, b)


def add_for_z(z, *pairs):
    def kernel(z_ref, *refs):
        terms, outs = refs[: 2 * len(pairs)], refs[2 * len(pairs) :]
        for d, o_ref in enumerate(outs):
            to = lax.rem(z_ref[0] + d, NZ)
            at = 0
            for a_ref, b_ref in zip(terms[0::2], terms[1::2]):
                n = a_ref.shape[1]
                o_ref[at : at + n] = a_ref[to] + b_ref[to]
                at += n

    held = sum(p[0].shape[1] for p in pairs)
    out = jax.ShapeDtypeStruct((held, ROWS, TILE), pairs[0][0].dtype)
    in_vmem = pl.BlockSpec(memory_space=pltpu.VMEM)
    return pl.pallas_call(
        kernel,
        out_shape=(out,) * NZ,
        in_specs=[pl.BlockSpec(memory_space=pltpu.SMEM)] + [in_vmem] * (2 * len(pairs)),
        out_specs=(in_vmem,) * NZ,
        compiler_params=pltpu.CompilerParams(vmem_limit_bytes=16 * 1024 * 1024),
        cost_estimate=SHORT,
        name="add_for_z",
    )(z, *[v for p in pairs for v in p])


def add_pairs(*pairs):
    def kernel(*refs):
        n = len(pairs)
        for i in range(n):
            refs[2 * n + i][...] = refs[2 * i][...] + refs[2 * i + 1][...]

    out = tuple(jax.ShapeDtypeStruct(p[0].shape, p[0].dtype) for p in pairs)
    return small_call(kernel, out, "add_pairs")(*[v for p in pairs for v in p])


def matmul_kernel(nb, per_block, core_ref, a_ref, *refs):
    n = nb * per_block
    pieces, (mine, other) = refs[:n], refs[n:]
    first_core = core_ref[0] == 0
    rows, depth = a_ref.shape
    step = STEP * TILE
    span = depth // per_block
    for i in range(rows // step):
        for j in range(0, nb, 2):
            width = min(2, nb - j)
            acc = None
            for p in range(per_block):
                right = [pieces[per_block * (j + w) + p][...] for w in range(width)]
                right = right[0] if width == 1 else jnp.concatenate(right, axis=1)
                part = jnp.dot(
                    a_ref[i * step : (i + 1) * step, p * span : (p + 1) * span],
                    right,
                    preferred_element_type=jnp.float32,
                )
                acc = part if acc is None else acc + part
            for w in range(width):
                halves = acc[:, w * TILE : (w + 1) * TILE].reshape(STEP, 2, NZ, ROWS, TILE)
                for t in range(STEP):
                    kept = jnp.where(first_core, halves[t, 0], halves[t, 1])
                    sent = jnp.where(first_core, halves[t, 1], halves[t, 0])
                    at = i * STEP + t
                    mine[:, j + w, at] = kept
                    other[:, j + w, at] = sent


def matmul(core, a, blocks, cost):
    tiles = a.shape[0] // TILE
    nb, per_block = len(blocks), len(blocks[0])
    arrays = [v for b in blocks for v in b]
    out = jax.ShapeDtypeStruct((NZ, nb, tiles, ROWS, TILE), jnp.float32)
    in_vmem = pl.BlockSpec(memory_space=pltpu.VMEM)
    return pl.pallas_call(
        functools.partial(matmul_kernel, nb, per_block),
        out_shape=(out, out),
        in_specs=[pl.BlockSpec(memory_space=pltpu.SMEM)] + [in_vmem] * (1 + len(arrays)),
        out_specs=(in_vmem, in_vmem),
        compiler_params=pltpu.CompilerParams(vmem_limit_bytes=18 * 1024 * 1024),
        cost_estimate=cost,
        name="tile_products",
    )(core, a, *arrays)


def place_kernel(index_ref, own1, pair1, own2, pair2, last, cross, out_ref, s):
    at = own1.shape[0]
    s[:at] = own1[...] + pair1[...]
    s[at:] = (own2[...] + last[...]) + (pair2[...] + cross[...])
    for d in range(out_ref.shape[0]):
        for k in range(0, CAP, 2):
            both = []
            for w in range(2):
                t = index_ref[d * CAP + k + w]
                value = s[jnp.maximum(t, 0)]
                both.append(jnp.where(t >= 0, value, jnp.zeros_like(value)))
            out_ref[d, k * ROWS : (k + 2) * ROWS, :] = jnp.concatenate(both, axis=0).astype(
                out_ref.dtype
            )


def place(index, parts, peers):
    held = parts[0].shape[0] + parts[2].shape[0]
    return pl.pallas_call(
        place_kernel,
        out_shape=jax.ShapeDtypeStruct((peers, CAP * ROWS, TILE), jnp.bfloat16),
        in_specs=[pl.BlockSpec(memory_space=pltpu.SMEM)]
        + [pl.BlockSpec(memory_space=pltpu.VMEM)] * len(parts),
        out_specs=pl.BlockSpec(memory_space=pltpu.VMEM),
        scratch_shapes=[pltpu.VMEM((held, ROWS, TILE), jnp.float32)],
        compiler_params=pltpu.CompilerParams(vmem_limit_bytes=8 * 1024 * 1024),
        name="place_tiles",
    )(index, *parts)


def placement(owner_map, row, y_lo, peers):
    count = owner_map.shape[1]
    owners = owner_map.reshape(count)
    number = jnp.arange(count, dtype=jnp.int32)
    earlier = (owners[None, :] == owners[:, None]) & (number[None, :] < number[:, None])
    slots = jnp.sum(earlier.astype(jnp.int32), axis=1)
    n_cols = len(ORDER)
    a, b = number // n_cols, number % n_cols
    n_rows = count // n_cols
    arrival = jnp.zeros_like(number)
    for j, (dx, dh) in enumerate(ORDER):
        col = 2 * ((row // 2 + dx + NX) % NX) + (row + dh) % 2
        arrival = arrival + jnp.where(b == col, j * n_rows + a, 0)
    wanted = y_lo * peers * CAP + jnp.arange(peers * CAP, dtype=jnp.int32)
    hit = (owners[None, :] * CAP + slots[None, :]) == wanted[:, None]
    return jnp.sum(jnp.where(hit, arrival[None, :] + 1, 0), axis=1).astype(jnp.int32) - 1


def per_device(integrals, density, mask_int, mask_den, owner_map):
    depth = density.shape[0]
    half = depth // 2
    k_tiles = depth // TILE
    layer = lax.axis_index("layer")
    row = lax.axis_index("row")
    y_lo = layer // 2
    z = lax.axis_index("col").astype(jnp.int32).reshape(1)
    core = (layer % 2).astype(jnp.int32).reshape(1)
    hold = lax.optimization_barrier

    scale = mask_den.astype(jnp.bfloat16)[:, :, None]
    own = (density.reshape(k_tiles, TILE, TILE) * scale).reshape(depth, TILE)

    def products(blocks, cost):
        return matmul(core, masked, blocks, cost)

    def core_swap(v):
        return lax.ppermute(v, "layer", CORE_SWAP)

    def y_swap(v):
        return lax.ppermute(v, "layer", YLO_SWAP)

    def to_z(chip):
        return lax.all_to_all(chip, "col", split_axis=0, concat_axis=0, tiled=True)

    def z_shift(v, step):
        return lax.ppermute(v, "col", [(i, (i + step) % NZ) for i in range(NZ)])

    def tiles(v):
        return v.reshape(NZ, -1, ROWS, TILE)

    l0, r0, p0 = from_left(own), from_right(own), from_pair(own)
    integrals, core, z = hold((integrals, core, z))
    masked = mask_rows(integrals, mask_int)
    mine0, other0 = products([(own,)], SHORT)
    came0 = core_swap(other0)
    l0, r0, p0, masked, mine0, came0 = hold((l0, r0, p0, masked, mine0, came0))
    l0a, l0b, r0b, p0a = split(l0, r0, p0)
    o0a, o0b, r1b = from_left(l0a), from_right(r0b), from_pair(r0b)
    mine1, other1 = products([(l0,), (r0,), (p0,)], LONG)
    o0a, o0b, r1b, l0b, p0a, mine1, other1 = hold((o0a, o0b, r1b, l0b, p0a, mine1, other1))
    l1a, r1a, l1b = from_left(p0a), from_right(p0a), from_pair(l0b)
    o1a, o1b = from_pair(o0a), from_right(r1b)
    chip1 = add(mine1, core_swap(other1))
    came1 = to_z(chip1)
    l1a, l1b, r1a, chip1 = hold((l1a, l1b, r1a, chip1))
    mine2, other2 = products([(o0a, o0b), (l1a, l1b)], LONG)
    o1a, o1b, mine2, other2 = hold((o1a, o1b, mine2, other2))
    mine3, other3 = products([(r1a, r1b), (o1a, o1b)], SHORT)
    by_z = add_for_z(
        z,
        (tiles(mine2), tiles(core_swap(other2))),
        (tiles(mine3), tiles(core_swap(other3))),
        (tiles(mine0), tiles(came0)),
    )
    owner_map, *by_z = hold((owner_map, *by_z))
    down, up = z_shift(by_z[4], -1), z_shift(by_z[3], 1)
    down, up = add_pairs((down, by_z[5]), (up, by_z[2]))
    down, up = z_shift(down, -1), z_shift(up, 1)
    down, up, came1 = hold((*add_pairs((down, by_z[6]), (up, by_z[1])), came1))
    down, up = z_shift(down, -1), z_shift(up, 1)
    share1 = jnp.sum(came1, axis=0).reshape(-1, ROWS, TILE)
    pair1 = y_swap(share1)
    down, share1 = hold((down, share1))
    (down,) = add_pairs((down, by_z[7]))
    over = [
        (i * NZ + k, (i ^ 2) * NZ + (k - 1) % NZ) for i in range(len(CORE_SWAP)) for k in range(NZ)
    ]
    last, cross = z_shift(down, -1), lax.ppermute(down, ("layer", "col"), over)
    rest = add(by_z[0], up)
    parts = share1, pair1, rest, y_swap(rest), last, cross

    peers = 2 * NZ
    outgoing = place(placement(owner_map, row, y_lo, peers), parts, peers)
    arrived = lax.all_to_all(
        outgoing,
        ("layer", "col"),
        split_axis=0,
        concat_axis=0,
        axis_index_groups=[list(range(peers)), list(range(peers, 2 * peers))],
        tiled=True,
    )
    placed = arrived.reshape(peers, CAP, ROWS, TILE).transpose(1, 0, 2, 3)
    return placed.reshape(1, 1, CAP, TILE, TILE)


def solution(mesh):
    placed = (
        P("row", ("layer", "col")),
        P(("layer", "col"), "row"),
        P("row", ("layer", "col")),
        P(("layer", "col"), "row"),
        P("row", None, None),
    )
    return jax.shard_map(
        per_device,
        mesh=mesh,
        in_specs=placed,
        out_specs=P("row", ("layer", "col"), None, None, None),
        check_vma=False,
    )
```

```python
import functools
import jax
import jax.numpy as jnp
from jax import lax
from jax.experimental import pallas as pl
from jax.experimental.pallas import tpu as pltpu
from jax.sharding import PartitionSpec as P

TILE = 128
CAP = 4
NX = 4
NZ = 8
ROWS = 8
STEP = 2
ORDER = [(-1, 0), (1, 0), (0, 1), (2, 0), (-1, 1), (1, 1), (2, 1), (0, 0)]


LONG = pl.CostEstimate(flops=10**11, bytes_accessed=10**8, transcendentals=0)
SHORT = pl.CostEstimate(flops=1000, bytes_accessed=1000, transcendentals=0)


def x_shift(step):
    return [(2 * x + h, 2 * ((x + step) % NX) + h) for x in range(NX) for h in range(2)]


Y_SWAP = [(2 * x + h, 2 * x + 1 - h) for x in range(NX) for h in range(2)]
CORE_SWAP = [(i, i ^ 1) for i in range(4)]
YLO_SWAP = [(i, i ^ 2) for i in range(4)]


def from_left(v):
    return lax.ppermute(v, "row", x_shift(1))


def from_right(v):
    return lax.ppermute(v, "row", x_shift(-1))


def from_pair(v):
    return lax.ppermute(v, "row", Y_SWAP)


def small_call(kernel, out_shape, name, limit=8):
    return pl.pallas_call(
        kernel,
        out_shape=out_shape,
        compiler_params=pltpu.CompilerParams(vmem_limit_bytes=limit * 1024 * 1024),
        cost_estimate=SHORT,
        name=name,
    )


def mask_rows(a, mask):
    rows, depth = a.shape
    by_row = jnp.repeat(mask.astype(jnp.bfloat16), TILE, axis=1)[:, None, :]

    def kernel(a_ref, m_ref, o_ref):
        at = pl.multiple_of(pl.program_id(0) * TILE, TILE)
        o_ref[pl.ds(at, TILE), :] = a_ref[...] * m_ref[0]

    return pl.pallas_call(
        kernel,
        out_shape=pltpu.VMEM(a.shape, a.dtype),
        grid=(rows // TILE,),
        in_specs=[
            pl.BlockSpec((TILE, depth), lambda i: (i, 0)),
            pl.BlockSpec((1, 1, depth), lambda i: (i, 0, 0)),
        ],
        out_specs=pl.BlockSpec(memory_space=pltpu.VMEM),
        compiler_params=pltpu.CompilerParams(vmem_limit_bytes=16 * 1024 * 1024),
        cost_estimate=SHORT,
        name="mask_integrals",
    )(a, by_row)


def halves(v, *which):
    half = v.shape[0] // 2

    def kernel(v_ref, *outs):
        for h, o_ref in zip(which, outs):
            o_ref[...] = v_ref[h * half : (h + 1) * half, :]

    out = jax.ShapeDtypeStruct((half, v.shape[1]), v.dtype)
    return small_call(kernel, (out,) * len(which), "halves")(v)


def add(a, b):
    def kernel(a_ref, b_ref, o_ref):
        o_ref[...] = a_ref[...] + b_ref[...]

    return small_call(kernel, jax.ShapeDtypeStruct(a.shape, a.dtype), "add_cores")(a, b)


def add_for_z(z, *pairs):
    def kernel(z_ref, *refs):
        terms, outs = refs[: 2 * len(pairs)], refs[2 * len(pairs) :]
        for d, o_ref in enumerate(outs):
            to = lax.rem(z_ref[0] + d, NZ)
            at = 0
            for a_ref, b_ref in zip(terms[0::2], terms[1::2]):
                n = a_ref.shape[1]
                o_ref[at : at + n] = a_ref[to] + b_ref[to]
                at += n

    held = sum(p[0].shape[1] for p in pairs)
    out = jax.ShapeDtypeStruct((held, ROWS, TILE), pairs[0][0].dtype)
    in_vmem = pl.BlockSpec(memory_space=pltpu.VMEM)
    return pl.pallas_call(
        kernel,
        out_shape=(out,) * NZ,
        in_specs=[pl.BlockSpec(memory_space=pltpu.SMEM)] + [in_vmem] * (2 * len(pairs)),
        out_specs=(in_vmem,) * NZ,
        compiler_params=pltpu.CompilerParams(vmem_limit_bytes=16 * 1024 * 1024),
        cost_estimate=SHORT,
        name="add_for_z",
    )(z, *[v for p in pairs for v in p])


def add_pairs(*pairs):
    def kernel(*refs):
        n = len(pairs)
        for i in range(n):
            refs[2 * n + i][...] = refs[2 * i][...] + refs[2 * i + 1][...]

    out = tuple(jax.ShapeDtypeStruct(p[0].shape, p[0].dtype) for p in pairs)
    return small_call(kernel, out, "add_pairs")(*[v for p in pairs for v in p])


def matmul_kernel(nb, per_block, core_ref, a_ref, *refs):
    n = nb * per_block
    pieces, (mine, other) = refs[:n], refs[n:]
    first_core = core_ref[0] == 0
    rows, depth = a_ref.shape
    step = STEP * TILE
    span = depth // per_block
    for i in range(rows // step):
        for j in range(0, nb, 2):
            width = min(2, nb - j)
            acc = None
            for p in range(per_block):
                right = [pieces[per_block * (j + w) + p][...] for w in range(width)]
                right = right[0] if width == 1 else jnp.concatenate(right, axis=1)
                part = jnp.dot(
                    a_ref[i * step : (i + 1) * step, p * span : (p + 1) * span],
                    right,
                    preferred_element_type=jnp.float32,
                )
                acc = part if acc is None else acc + part
            for w in range(width):
                halves = acc[:, w * TILE : (w + 1) * TILE].reshape(STEP, 2, NZ, ROWS, TILE)
                for t in range(STEP):
                    kept = jnp.where(first_core, halves[t, 0], halves[t, 1])
                    sent = jnp.where(first_core, halves[t, 1], halves[t, 0])
                    at = i * STEP + t
                    mine[:, j + w, at] = kept
                    other[:, j + w, at] = sent


def matmul(core, a, blocks, cost):
    tiles = a.shape[0] // TILE
    nb, per_block = len(blocks), len(blocks[0])
    arrays = [v for b in blocks for v in b]
    out = jax.ShapeDtypeStruct((NZ, nb, tiles, ROWS, TILE), jnp.float32)
    in_vmem = pl.BlockSpec(memory_space=pltpu.VMEM)
    return pl.pallas_call(
        functools.partial(matmul_kernel, nb, per_block),
        out_shape=(out, out),
        in_specs=[pl.BlockSpec(memory_space=pltpu.SMEM)] + [in_vmem] * (1 + len(arrays)),
        out_specs=(in_vmem, in_vmem),
        compiler_params=pltpu.CompilerParams(vmem_limit_bytes=18 * 1024 * 1024),
        cost_estimate=cost,
        name="tile_products",
    )(core, a, *arrays)


def place_kernel(index_ref, own1, pair1, own2, pair2, last, cross, out_ref, s):
    at = own1.shape[0]
    s[:at] = own1[...] + pair1[...]
    s[at:] = (own2[...] + last[...]) + (pair2[...] + cross[...])
    for d in range(out_ref.shape[0]):
        for k in range(0, CAP, 2):
            both = []
            for w in range(2):
                t = index_ref[d * CAP + k + w]
                value = s[jnp.maximum(t, 0)]
                both.append(jnp.where(t >= 0, value, jnp.zeros_like(value)))
            out_ref[d, k * ROWS : (k + 2) * ROWS, :] = jnp.concatenate(both, axis=0).astype(
                out_ref.dtype
            )


def place(index, parts, peers):
    held = parts[0].shape[0] + parts[2].shape[0]
    return pl.pallas_call(
        place_kernel,
        out_shape=jax.ShapeDtypeStruct((peers, CAP * ROWS, TILE), jnp.bfloat16),
        in_specs=[pl.BlockSpec(memory_space=pltpu.SMEM)]
        + [pl.BlockSpec(memory_space=pltpu.VMEM)] * len(parts),
        out_specs=pl.BlockSpec(memory_space=pltpu.VMEM),
        scratch_shapes=[pltpu.VMEM((held, ROWS, TILE), jnp.float32)],
        compiler_params=pltpu.CompilerParams(vmem_limit_bytes=8 * 1024 * 1024),
        name="place_tiles",
    )(index, *parts)


def placement(owner_map, row, y_lo, peers):
    count = owner_map.shape[1]
    owners = owner_map.reshape(count)
    number = jnp.arange(count, dtype=jnp.int32)
    earlier = (owners[None, :] == owners[:, None]) & (number[None, :] < number[:, None])
    slots = jnp.sum(earlier.astype(jnp.int32), axis=1)
    n_cols = len(ORDER)
    a, b = number // n_cols, number % n_cols
    n_rows = count // n_cols
    arrival = jnp.zeros_like(number)
    for j, (dx, dh) in enumerate(ORDER):
        col = 2 * ((row // 2 + dx + NX) % NX) + (row + dh) % 2
        arrival = arrival + jnp.where(b == col, j * n_rows + a, 0)
    wanted = y_lo * peers * CAP + jnp.arange(peers * CAP, dtype=jnp.int32)
    hit = (owners[None, :] * CAP + slots[None, :]) == wanted[:, None]
    return jnp.sum(jnp.where(hit, arrival[None, :] + 1, 0), axis=1).astype(jnp.int32) - 1


def per_device(integrals, density, mask_int, mask_den, owner_map):
    depth = density.shape[0]
    half = depth // 2
    k_tiles = depth // TILE
    layer = lax.axis_index("layer")
    row = lax.axis_index("row")
    y_lo = layer // 2
    z = lax.axis_index("col").astype(jnp.int32).reshape(1)
    core = (layer % 2).astype(jnp.int32).reshape(1)
    hold = lax.optimization_barrier

    scale = mask_den.astype(jnp.bfloat16)[:, :, None]
    own = (density.reshape(k_tiles, TILE, TILE) * scale).reshape(depth, TILE)

    def products(blocks, cost):
        return matmul(core, masked, blocks, cost)

    def core_swap(v):
        return lax.ppermute(v, "layer", CORE_SWAP)

    def y_swap(v):
        return lax.ppermute(v, "layer", YLO_SWAP)

    def to_z(chip):
        return lax.all_to_all(chip, "col", split_axis=0, concat_axis=0, tiled=True)

    def z_shift(v, step):
        return lax.ppermute(v, "col", [(i, (i + step) % NZ) for i in range(NZ)])

    def tiles(v):
        return v.reshape(NZ, -1, ROWS, TILE)

    l0, r0, p0 = from_left(own), from_right(own), from_pair(own)
    integrals, core, z = hold((integrals, core, z))
    masked = mask_rows(integrals, mask_int)
    mine0, other0 = products([(own,)], SHORT)
    came0 = core_swap(other0)
    r0, masked, mine0, came0 = hold((r0, masked, mine0, came0))
    (r0b,) = halves(r0, 1)
    l0, masked = hold((l0, masked))
    l0a, l0b = halves(l0, 0, 1)
    p0, masked = hold((p0, masked))
    (p0a,) = halves(p0, 0)
    o0a, o0b, r1b = from_left(l0a), from_right(r0b), from_pair(r0b)
    mine1, other1 = products([(l0,), (r0,), (p0,)], LONG)
    o0a, o0b, r1b, l0b, p0a, mine1, other1 = hold((o0a, o0b, r1b, l0b, p0a, mine1, other1))
    l1a, r1a, l1b = from_left(p0a), from_right(p0a), from_pair(l0b)
    o1a, o1b = from_pair(o0a), from_right(r1b)
    chip1 = add(mine1, core_swap(other1))
    came1 = to_z(chip1)
    l1a, l1b, r1a, chip1 = hold((l1a, l1b, r1a, chip1))
    mine2, other2 = products([(o0a, o0b), (l1a, l1b)], LONG)
    o1a, o1b, mine2, other2 = hold((o1a, o1b, mine2, other2))
    mine3, other3 = products([(r1a, r1b), (o1a, o1b)], SHORT)
    by_z = add_for_z(
        z,
        (tiles(mine2), tiles(core_swap(other2))),
        (tiles(mine3), tiles(core_swap(other3))),
        (tiles(mine0), tiles(came0)),
    )
    owner_map, *by_z = hold((owner_map, *by_z))
    down, up = z_shift(by_z[4], -1), z_shift(by_z[3], 1)
    down, up = add_pairs((down, by_z[5]), (up, by_z[2]))
    down, up = z_shift(down, -1), z_shift(up, 1)
    down, up, came1 = hold((*add_pairs((down, by_z[6]), (up, by_z[1])), came1))
    down, up = z_shift(down, -1), z_shift(up, 1)
    share1 = jnp.sum(came1, axis=0).reshape(-1, ROWS, TILE)
    pair1 = y_swap(share1)
    down, share1 = hold((down, share1))
    (down,) = add_pairs((down, by_z[7]))
    over = [
        (i * NZ + k, (i ^ 2) * NZ + (k - 1) % NZ) for i in range(len(CORE_SWAP)) for k in range(NZ)
    ]
    last, cross = z_shift(down, -1), lax.ppermute(down, ("layer", "col"), over)
    rest = add(by_z[0], up)
    parts = share1, pair1, rest, y_swap(rest), last, cross

    peers = 2 * NZ
    outgoing = place(placement(owner_map, row, y_lo, peers), parts, peers)
    arrived = lax.all_to_all(
        outgoing,
        ("layer", "col"),
        split_axis=0,
        concat_axis=0,
        axis_index_groups=[list(range(peers)), list(range(peers, 2 * peers))],
        tiled=True,
    )
    placed = arrived.reshape(peers, CAP, ROWS, TILE).transpose(1, 0, 2, 3)
    return placed.reshape(1, 1, CAP, TILE, TILE)


def solution(mesh):
    placed = (
        P("row", ("layer", "col")),
        P(("layer", "col"), "row"),
        P("row", ("layer", "col")),
        P(("layer", "col"), "row"),
        P("row", None, None),
    )
    return jax.shard_map(
        per_device,
        mesh=mesh,
        in_specs=placed,
        out_specs=P("row", ("layer", "col"), None, None, None),
        check_vma=False,
    )
```
